32 devices in a mesh: grp: 8 (over z, core), dev: 4 (over y, x).
Axes of the slice: x: 2, y: 2, z: 4, core: 2. Of those that a mesh axis runs over, the one named last changes fastest.
Arguments:
- voxel_features: float32 [128, 64, 512], P(('grp', 'dev')), may hold values from -6 to 6
- fine_links: int32 [128, 26], P(('grp', 'dev')), may hold values from -1 to 127, as said below
- parent_codes: int32 [128], P(('grp', 'dev')), may hold values from 0 to 63, as said below
- coarse_links: int32 [64, 26], P(('grp', 'dev')), may hold values from -1 to 63, as said below
- fine_in_weight: float32 [64, 1728], replicated, may hold values from -0.15625 to 0.15625
- fine_in_bias: float32 [64], replicated, may hold values from -3 to 3
- down_weight: float32 [128, 64], replicated, may hold values from -0.75 to 0.75
- coarse_first_weight: float32 [128, 3456], replicated, may hold values from -0.109375 to 0.109375
- coarse_first_bias: float32 [128], replicated, may hold values from -3 to 3
- coarse_second_weight: float32 [128, 3456], replicated, may hold values from -0.109375 to 0.109375
- coarse_second_bias: float32 [128], replicated, may hold values from -3 to 3
- up_weight: float32 [64, 128], replicated, may hold values from -0.5 to 0.5
- fine_out_weight: float32 [64, 1728], replicated, may hold values from -0.15625 to 0.15625
- fine_out_bias: float32 [64], replicated, may hold values from -3 to 3
Outputs:
- refined: float32 [128, 64, 512], P(('grp', 'dev'))
The draws below stay inside these ranges and needn't reach their ends.
Inputs may be any that keep to these rules, and one draw needn't show every extreme that they name: `fine_links`: devices are numbered along grp then dev, device d holding bricks d * 4 to (d + 1) * 4 - 1. An entry is -1 or a brick from d * 4 - 2 to (d + 1) * 4 + 1 for a brick of device d, with 2 = 2. parent_codes[i] = 8 * 2 * owner + 8 * slot + octant: owner is the dev index, within the brick's group of 4 devices, of the device that holds the parent, slot the parent's slot there (0 to 1), and octant = 4 * a + 2 * b + c the child's octant. Within a group all codes differ; the number of slots in use differs from device to device, and some device of every group uses all 2. `coarse_links`: device d holds slots d * 2 to (d + 1) * 2 - 1. An entry is -1 or a slot from (d - 1) * 2 to (d + 2) * 2 - 1 for a slot of device d.
All inputs are finite; a program needn't handle non-finite values.
Results may differ from the reference program's by a relative error of at most 0.0001.
Values sent between devices are 32-bit elements; how exact they have to be, the bound alone decides.
A program may use at most 128 MiB of HBM per device.

```python
import jax
import jax.numpy as jnp
from jax import lax

CF = 64
CC = 128
BR = 4
CMAX = 2
HALO = 2
NB = 128
NCS = 64
N_GRP = 8
N_DEV = 4


def nearby_links(key, row_total, run_length, reach_low, reach_high):
    positions = jnp.arange(row_total, dtype=jnp.int32)
    first_slot = positions // run_length * run_length
    key_offset, key_keep = jax.random.split(key)
    offsets = jax.random.randint(key_offset, (row_total, 26), -reach_low, run_length + reach_high, dtype=jnp.int32)
    targets = jnp.clip(first_slot[:, None] + offsets, 0, row_total - 1)
    kept_mask = jax.random.randint(key_keep, (row_total, 26), 0, 10, dtype=jnp.int32) < 7
    return jnp.where(kept_mask, targets, -1).astype(jnp.int32)


def draw_fine_links(key, part):
    return nearby_links(jax.random.fold_in(key, 11), NB, BR, HALO, HALO)


def draw_coarse_links(key, part):
    return nearby_links(jax.random.fold_in(key, 12), NCS, CMAX, CMAX, CMAX)


def draw_parent_codes(key, part):
    key_live, key_pick, key_score = jax.random.split(jax.random.fold_in(key, 13), 3)
    fewest = (BR + 7) // 8
    live_slots = jax.random.randint(key_live, (N_GRP, N_DEV), fewest, CMAX + 1, dtype=jnp.int32)
    chosen = jax.random.randint(key_pick, (N_GRP, 1), 0, N_DEV, dtype=jnp.int32)
    live_slots = jnp.where(jnp.arange(N_DEV, dtype=jnp.int32)[None, :] == chosen, CMAX, live_slots)
    code_total = N_DEV * CMAX * 8
    code_ids = jnp.arange(code_total, dtype=jnp.int32)
    owners = code_ids // (CMAX * 8)
    slot_ids = code_ids // 8 % CMAX
    alive_codes = slot_ids[None, :] < live_slots[:, owners]
    scores = jax.random.randint(key_score, (N_GRP, code_total), 0, 2 ** 20, dtype=jnp.int32)
    scores = scores + jnp.where(alive_codes, 0, 2 ** 21)
    ranked = jnp.argsort(scores * code_total + code_ids[None, :], axis=1)
    return ranked[:, :N_DEV * BR].reshape(-1).astype(jnp.int32)


def levels(stream_key, dims, cuts, low, largest):
    loudness = 1.0
    for axis_at, blocks in cuts:
        steps = jax.random.uniform(jax.random.fold_in(jax.random.fold_in(stream_key, 6), axis_at), (blocks,), jnp.float32, low / len(cuts), largest / len(cuts))
        loudness = loudness * jnp.repeat(jnp.exp(steps), dims[axis_at] // blocks).reshape((-1,) + (1,) * (len(dims) - 1 - axis_at))
    return loudness


def scatter_about(rng, shape, spread, reach, cuts=(), kind=jnp.bfloat16):
    array = jax.random.normal(rng, shape, jnp.float32) * spread
    if len(cuts) > 0:
        array = levels(rng, shape, cuts, -0.22, 0.18) * array
    return jnp.clip(array, min=-reach, max=reach).astype(kind)


def setup_inputs(seed: int = 0) -> dict:
    key_list = jax.random.split(jax.random.key(seed), 15)
    voxel_features = scatter_about(key_list[0], (NB, CF, 512), 1.0, 6.0, ((0, 32),), jnp.float32)
    fine_links = draw_fine_links(jax.random.fold_in(key_list[14], 71), 0)
    parent_codes = draw_parent_codes(jax.random.fold_in(key_list[14], 71), 0)
    coarse_links = draw_coarse_links(jax.random.fold_in(key_list[14], 71), 0)
    fine_in_weight = scatter_about(key_list[4], (CF, 27 * CF), (27 * CF) ** -0.5, 0.15625, (), jnp.float32)
    fine_in_bias = scatter_about(key_list[5], (CF,), 0.5, 3.0, (), jnp.float32)
    down_weight = scatter_about(key_list[6], (CC, CF), CF ** -0.5, 0.75, (), jnp.float32)
    coarse_first_weight = scatter_about(key_list[7], (CC, 27 * CC), (27 * CC) ** -0.5, 0.109375, (), jnp.float32)
    coarse_first_bias = scatter_about(key_list[8], (CC,), 0.5, 3.0, (), jnp.float32)
    coarse_second_weight = scatter_about(key_list[9], (CC, 27 * CC), (27 * CC) ** -0.5, 0.109375, (), jnp.float32)
    coarse_second_bias = scatter_about(key_list[10], (CC,), 0.5, 3.0, (), jnp.float32)
    up_weight = scatter_about(key_list[11], (CF, CC), CC ** -0.5, 0.5, (), jnp.float32)
    fine_out_weight = scatter_about(key_list[12], (CF, 27 * CF), (27 * CF) ** -0.5, 0.15625, (), jnp.float32)
    fine_out_bias = scatter_about(key_list[13], (CF,), 0.5, 3.0, (), jnp.float32)
    return {"voxel_features": voxel_features, "fine_links": fine_links, "parent_codes": parent_codes, "coarse_links": coarse_links, "fine_in_weight": fine_in_weight, "fine_in_bias": fine_in_bias, "down_weight": down_weight, "coarse_first_weight": coarse_first_weight, "coarse_first_bias": coarse_first_bias, "coarse_second_weight": coarse_second_weight, "coarse_second_bias": coarse_second_bias, "up_weight": up_weight, "fine_out_weight": fine_out_weight, "fine_out_bias": fine_out_bias}


neighbour_offsets = [(step_x, step_y, step_z) for step_x in (-1, 0, 1) for step_y in (-1, 0, 1) for step_z in (-1, 0, 1) if (step_x, step_y, step_z) != (0, 0, 0)]
source_planes = {-1: slice(7, 8), 0: slice(0, 8), 1: slice(0, 1)}


def assemble(source, center, links):
    extent = source.shape[0]
    bricks = center.shape[0]
    channels = center.shape[1]
    bricks_ext = jnp.concatenate([source, jnp.zeros((1,) + source.shape[1:], source.dtype)], 0)
    bricks_ext = bricks_ext.reshape(extent + 1, channels, 8, 8, 8)
    picked = jnp.where(links < 0, extent, links).astype(jnp.int32)
    middle = center.reshape(bricks, channels, 8, 8, 8)
    slabs = []
    for step_x in (-1, 0, 1):
        rows = []
        for step_y in (-1, 0, 1):
            cells = []
            for step_z in (-1, 0, 1):
                if (step_x, step_y, step_z) == (0, 0, 0):
                    cells.append(middle)
                else:
                    column = neighbour_offsets.index((step_x, step_y, step_z))
                    planes = bricks_ext[:, :, source_planes[step_x], source_planes[step_y], source_planes[step_z]]
                    cells.append(planes[picked[:, column]])
            rows.append(jnp.concatenate(cells, axis=4))
        slabs.append(jnp.concatenate(rows, axis=3))
    return jnp.concatenate(slabs, axis=2)


def convolve(source, center, links, weight, biases):
    padded = assemble(source, center, links)
    bricks = center.shape[0]
    channels = center.shape[1]
    summed = jnp.zeros((bricks, weight.shape[0], 512), jnp.float32)
    for offset_x in range(3):
        windows = []
        for offset_y in range(3):
            for offset_z in range(3):
                windows.append(padded[:, :, offset_x:offset_x + 8, offset_y:offset_y + 8, offset_z:offset_z + 8].reshape(bricks, channels, 512))
        stacked = jnp.concatenate(windows, axis=1)
        kernel = weight[:, 9 * offset_x * channels:(9 * offset_x + 9) * channels]
        summed = summed + jnp.einsum("oc,bcv->bov", kernel, stacked, precision=lax.Precision.HIGHEST)
    return summed + biases[None, :, None]


def pooling(hidden):
    bricks = hidden.shape[0]
    channels = hidden.shape[1]
    return hidden.reshape(bricks, channels, 4, 2, 4, 2, 4, 2).sum(axis=(3, 5, 7)).reshape(bricks, channels * 64) * 0.125


def octants_to_bricks(pieces, channels):
    slots = pieces.shape[0] // 8
    return pieces.reshape(slots, 2, 2, 2, channels, 4, 4, 4).transpose(0, 4, 1, 5, 2, 6, 3, 7).reshape(slots, channels, 512)


def bricks_to_octants(cubes, channels):
    slots = cubes.shape[0]
    return cubes.reshape(slots, channels, 2, 4, 2, 4, 2, 4).transpose(0, 2, 4, 6, 1, 3, 5, 7).reshape(slots * 8, channels * 64)


def upsample(octants, channels):
    bricks = octants.shape[0]
    grown = jnp.broadcast_to(octants.reshape(bricks, channels, 4, 1, 4, 1, 4, 1), (bricks, channels, 4, 2, 4, 2, 4, 2))
    return grown.reshape(bricks, channels, 512)


def reference(voxel_features, fine_links, parent_codes, coarse_links, fine_in_weight, fine_in_bias, down_weight, coarse_first_weight, coarse_first_bias, coarse_second_weight, coarse_second_bias, up_weight, fine_out_weight, fine_out_bias):
    bricks = voxel_features.shape[0]
    channels = voxel_features.shape[1]
    hidden = jax.nn.silu(convolve(voxel_features, voxel_features, fine_links, fine_in_weight, fine_in_bias))
    pooled = pooling(hidden)
    groups = jnp.arange(bricks, dtype=jnp.int32) // (N_DEV * BR)
    parent_rows = (groups * (N_DEV * CMAX * 8) + parent_codes.astype(jnp.int32)).astype(jnp.int32)
    slot_total = coarse_links.shape[0]
    pieces = jnp.zeros((slot_total * 8, channels * 64), jnp.float32).at[parent_rows].set(pooled)
    coarse_in = octants_to_bricks(pieces, channels)
    coarse_base = jnp.einsum("oc,bcv->bov", down_weight, coarse_in, precision=lax.Precision.HIGHEST)
    coarse_first = jax.nn.silu(convolve(coarse_base, coarse_base, coarse_links, coarse_first_weight, coarse_first_bias))
    coarse_second = jax.nn.silu(convolve(coarse_first, coarse_first, coarse_links, coarse_second_weight, coarse_second_bias))
    lifted = jnp.einsum("oc,bcv->bov", up_weight, coarse_second, precision=lax.Precision.HIGHEST)
    upward = bricks_to_octants(lifted, channels)
    rising = upsample(upward[parent_rows], channels)
    blended = jax.nn.silu(hidden + rising)
    return voxel_features + convolve(blended, blended, fine_links, fine_out_weight, fine_out_bias)
```

```python
import functools

import jax
import jax.numpy as jnp
from jax import lax
from jax.experimental import pallas as pl
from jax.experimental.pallas import tpu as pltpu
from jax.sharding import PartitionSpec as P

F32 = jnp.float32
BF16 = jnp.bfloat16
MESH = pl.DeviceIdType.MESH
SIDE = 8
VOX = SIDE * SIDE * SIDE
OCT = VOX // 8
PADDED = SIDE + 2
HALO = 2
LIMIT = 60 * 1024 * 1024

offsets = [(x, y, z) for x in (-1, 0, 1) for y in (-1, 0, 1) for z in (-1, 0, 1)]
columns = {o: k for k, o in enumerate(o for o in offsets if o != (0, 0, 0))}
source = {-1: slice(7, 8), 0: slice(0, 8), 1: slice(0, 1)}
target = {-1: slice(0, 1), 0: slice(1, 9), 1: slice(9, 10)}


def split(v):
    high = v.astype(BF16).astype(F32)
    return high, v - high


def silu(v):
    return v / (1.0 + jnp.exp(-v))


def product(a, b, dims=((1,), (1,))):
    return lax.dot_general(a, b, (dims, ((), ())), preferred_element_type=F32)


def precise(a, b, dims=((1,), (1,))):
    return lax.dot_general(
        a, b, (dims, ((), ())), preferred_element_type=F32, precision=lax.Precision.HIGHEST
    )


def spread(v):
    half = v.shape[0] // 2
    return jnp.concatenate([v[:half], v[half:]], axis=1)


def unspread(v):
    width = v.shape[1] // 2
    return jnp.concatenate([v[:, :width], v[:, width:]], axis=0)


def put_parts(parts, index, v):
    high, low = split(v)
    parts[index] = jnp.concatenate([high, low], axis=1).reshape(SIDE, SIDE, SIDE, 2 * v.shape[1])


def fill(parts, own, start, links, brick, padded):
    for dx, dy, dz in offsets:
        spot = (dz + 1, target[dx], target[dy])
        if (dx, dy, dz) == (0, 0, 0):
            padded[spot] = parts[own]
            continue
        link = links[brick, columns[dx, dy, dz]]
        found = link >= 0
        row = jnp.where(found, link - start, own)
        keep = jnp.where(found, 1.0, 0.0).astype(F32)
        padded[spot] = parts[row, source[dx], source[dy]] * keep


def unfold(padded, patches):
    width = padded.shape[-1]
    z_at = lax.broadcasted_iota(jnp.int32, (PADDED, SIDE, width), 1)
    for x in range(PADDED):
        middle = padded[1, x]
        padded[0, x] = pltpu.roll(jnp.where(z_at == SIDE - 1, padded[0, x], middle), 1, 1)
        padded[2, x] = pltpu.roll(jnp.where(z_at == 0, padded[2, x], middle), SIDE - 1, 1)
    for i in range(3):
        for j in range(3):
            for k in range(3):
                tap = 9 * i + 3 * j + k
                window = padded[k, i : i + SIDE, j : j + SIDE].reshape(VOX, width)
                patches[:, tap * width : (tap + 1) * width] = window.astype(BF16)


def fine_matrix(weight, matrix):
    channels = weight.shape[0]
    lane = lax.broadcasted_iota(jnp.int32, (channels, 2 * channels), 1)
    for pair in range(14):
        if pair < 13:
            tile = weight[:, pair * 2 * channels : (pair + 1) * 2 * channels]
            turned = pltpu.roll(tile, channels, 1)
            taps = [
                jnp.where(lane < channels, tile, turned),
                jnp.where(lane < channels, turned, tile),
            ]
        else:
            tile = weight[:, 26 * channels : 27 * channels]
            taps = [jnp.concatenate([tile, tile], axis=1)]
        for at, tap in enumerate(taps):
            high, low = split(tap)
            cols = slice((2 * pair + at) * 2 * channels, (2 * pair + at + 1) * 2 * channels)
            matrix[0:channels, cols] = high.astype(BF16)
            matrix[channels : 2 * channels, cols] = low.astype(BF16)


def coarse_matrix(weight, matrix):
    channels = weight.shape[0]
    for tap in range(27):
        high, low = split(weight[:, tap * channels : (tap + 1) * channels])
        for part in range(2):
            cols = slice((2 * tap + part) * channels, (2 * tap + part + 1) * channels)
            matrix[0:channels, cols] = high.astype(BF16)
            matrix[channels : 2 * channels, cols] = low.astype(BF16)


def convolved(parts, own, start, links, brick, padded, patches, matrix, bias):
    fill(parts, own, start, links, brick, padded)
    unfold(padded, patches)
    both = product(patches[...], matrix[...])
    channels = both.shape[1] // 2
    return both[:, :channels] + both[:, channels:] + bias[...]


def place():
    return lax.axis_index("grp"), lax.axis_index("dev"), lax.axis_size("grp"), lax.axis_size("dev")


def first_kernel(x, left, right, links, weight, bias, hidden, pooled, parts, padded, patches, matrix):
    group, member, _, members = place()
    count = x.shape[0]
    start = (group * members + member) * count - HALO
    for i in range(count):
        put_parts(parts, HALO + i, x[i].T)
    for i in range(HALO):
        put_parts(parts, i, left[i].T)
        put_parts(parts, HALO + count + i, right[i].T)
    fine_matrix(weight, matrix)
    row = lax.broadcasted_iota(jnp.int32, (OCT, VOX), 0)
    col = lax.broadcasted_iota(jnp.int32, (OCT, VOX), 1)
    cell = (col // 128) * 16 + (col // 16 % 4) * 4 + col // 2 % 4
    pooling = jnp.where(row == cell, 0.125, 0.0).astype(BF16)

    def step(i, carry):
        out = silu(
            convolved(parts, HALO + i, start, links, i, padded, patches, matrix, bias)
        )
        hidden[i] = spread(out)
        high, low = split(out)
        both = jnp.concatenate([high, low], axis=1).astype(BF16)
        sums = product(pooling, both, ((1,), (0,)))
        width = out.shape[1]
        pooled[i] = spread(sums[:, :width] + sums[:, width:])
        return carry

    lax.fori_loop(0, count, step, 0)


def octant_order(flip):
    row = lax.broadcasted_iota(jnp.int32, (VOX, VOX), 1 if flip else 0)
    col = lax.broadcasted_iota(jnp.int32, (VOX, VOX), 0 if flip else 1)
    x, y, z = row // 64, row // 8 % 8, row % 8
    spot = (x // 4 * 4 + y // 4 * 2 + z // 4) * 64 + x % 4 * 16 + y % 4 * 4 + z % 4
    return jnp.where(spot == col, 1.0, 0.0).astype(BF16)


def second_kernel(pooled, codes, links, down, weight, bias, first, pieces, parts, padded, patches, matrix):
    group, member, groups, members = place()
    slots = links.shape[0]
    count = pooled.shape[1]
    start = (group * members + member - 1) * slots
    position = group * members + member
    pieces[...] = jnp.zeros_like(pieces)
    coarse_matrix(weight, matrix)
    for near in range(3):
        there = position + near - 1
        there_group = (there + members) // members - 1
        there_member = there - there_group * members
        band = there_group - group + 1
        valid = (there >= 0) & (there < groups * members)
        for one in range(count):

            def visit(owner, carry):
                code = codes[(band * members + owner) * 8, one] - there_member * slots * 8

                @pl.when(valid & (code >= 0) & (code < slots * 8))
                def _():
                    pieces[near * slots * 8 + code] = unspread(
                        pooled[band * members + owner, one]
                    )

                return carry

            lax.fori_loop(0, members, visit, 0)
    order = octant_order(False)

    def base(slot, carry):
        piece = pieces[pl.ds(slot * 8, 8)].reshape(VOX, pieces.shape[-1])
        lifted = precise(piece, down[...])
        high, low = split(lifted)
        both = jnp.concatenate([high, low], axis=1).astype(BF16)
        parts[slot] = product(order, both, ((1,), (0,))).reshape(SIDE, SIDE, SIDE, both.shape[1])
        return carry

    lax.fori_loop(0, 3 * slots, base, 0)

    def step(i, carry):
        first[i] = silu(
            convolved(parts, slots + i, start, links, i, padded, patches, matrix, bias)
        )
        return carry

    lax.fori_loop(0, slots, step, 0)


def third_kernel(first, left, right, links, weight, bias, up, lifted, parts, padded, patches, matrix):
    group, member, _, members = place()
    slots = links.shape[0]
    start = (group * members + member - 1) * slots
    coarse_matrix(weight, matrix)
    for i in range(slots):
        put_parts(parts, i, left[i])
        put_parts(parts, slots + i, first[i])
        put_parts(parts, 2 * slots + i, right[i])
    order = octant_order(True)

    def step(i, carry):
        out = silu(
            convolved(parts, slots + i, start, links, i, padded, patches, matrix, bias)
        )
        high, low = split(precise(out, up[...]))
        both = jnp.concatenate([high, low], axis=1).astype(BF16)
        sums = product(order, both, ((1,), (0,)))
        width = high.shape[1]
        ordered = sums[:, :width] + sums[:, width:]
        for octant in range(8):
            lifted[i * 8 + octant] = spread(ordered[octant * OCT : (octant + 1) * OCT])
        return carry

    lax.fori_loop(0, slots, step, 0)


def fourth_kernel(x, hidden, left, right, lifted, codes, links, weight, bias, out, parts, padded, patches, matrix):
    group, member, groups, members = place()
    count = x.shape[0]
    start = (group * members + member) * count - HALO
    fine_matrix(weight, matrix)
    row = lax.broadcasted_iota(jnp.int32, (VOX, OCT), 0)
    col = lax.broadcasted_iota(jnp.int32, (VOX, OCT), 1)
    cell = (row // 128) * 16 + (row // 16 % 4) * 4 + row // 2 % 4
    repeat = jnp.where(col == cell, 1.0, 0.0).astype(BF16)
    octants = lifted.shape[1]
    for i in range(count + 2 * HALO):
        if i < HALO:
            before, one, held = -1, count - HALO + i, left[i]
        elif i < HALO + count:
            before, one, held = 0, i - HALO, hidden[i - HALO]
        else:
            before, one, held = 1, i - HALO - count, right[i - HALO - count]
        there = jnp.clip(group * members + member + before, 0, groups * members - 1)
        there_group = there // members
        there_member = there - there_group * members
        band = there_group - group + 1
        code = codes[(band * members + there_member) * 8, one]
        piece = unspread(lifted[band * members + code // octants, code % octants])
        high, low = split(piece)
        both = jnp.concatenate([high, low], axis=1).astype(BF16)
        sums = product(repeat, both, ((1,), (0,)))
        width = high.shape[1]
        put_parts(parts, i, silu(unspread(held) + sums[:, :width] + sums[:, width:]))

    def step(i, carry):
        conv = convolved(parts, HALO + i, start, links, i, padded, patches, matrix, bias)
        out[i] = x[i] + conv.T
        return carry

    lax.fori_loop(0, count, step, 0)


def exchange_kernel(margins, shared, *refs):
    halos = len(margins)
    total = halos + shared
    ins, outs = refs[:total], refs[total : total + 2 * halos + shared]
    send_halo, recv_halo, send_all, recv_all = refs[total + 2 * halos + shared :]
    group, member, groups, members = place()
    position = group * members + member
    whole = groups * members
    has_left, has_right = position > 0, position < whole - 1
    has_low, has_high = group > 0, group < groups - 1
    left_at = (jnp.maximum(position - 1, 0) // members, (position + members - 1) % members)
    right_at = (jnp.minimum(position + 1, whole - 1) // members, (position + 1) % members)
    low_at = (jnp.maximum(group - 1, 0), members - 1)
    high_at = (jnp.minimum(group + 1, groups - 1), 0)

    barrier = pltpu.get_barrier_semaphore()

    def greet(where):
        pl.semaphore_signal(barrier, inc=1, device_id=where, device_id_type=MESH)

    count = jnp.int32(0)
    if halos:
        pl.when(has_left)(lambda: greet(left_at))
        pl.when(has_right)(lambda: greet(right_at))
        count = count + jnp.where(has_left, 1, 0) + jnp.where(has_right, 1, 0)
    if shared:
        for k in range(1, members):
            greet((group, (member + k) % members))
        for k in range(members):
            pl.when((member == 0) & has_low)(lambda k=k: greet((low_at[0], k)))
            pl.when((member == members - 1) & has_high)(lambda k=k: greet((high_at[0], k)))
        count = count + (members - 1) + jnp.where(has_low, 1, 0) + jnp.where(has_high, 1, 0)
    pl.semaphore_wait(barrier, count)

    def remote(src, dst, send, recv, where):
        return pltpu.make_async_remote_copy(
            src_ref=src, dst_ref=dst, send_sem=send, recv_sem=recv,
            device_id=where, device_id_type=MESH,
        )

    def each(action):
        for a in range(shared):
            src, out = ins[halos + a], outs[2 * halos + a]
            for k in range(1, members):
                spot = members + (member if action == "start" else (member + k) % members)
                copy = remote(
                    src, out.at[spot], send_all.at[a, k], recv_all.at[a, spot],
                    (group, (member + k) % members),
                )
                copy.start() if action == "start" else copy.wait()

            def across(where, base, lane, a=a, src=src, out=out):
                remote(
                    src, out.at[base + member], send_all.at[a, lane],
                    recv_all.at[a, base + member], where,
                ).start()

            def ended(where, lane, a=a, src=src, out=out):
                remote(
                    src, out.at[member], send_all.at[a, lane], recv_all.at[a, member], where
                ).wait_send()

            def arrived(spot, where, a=a, src=src, out=out):
                remote(
                    src, out.at[spot], send_all.at[a, 0], recv_all.at[a, spot], where
                ).wait_recv()

            if action == "start":
                pl.when(has_high)(lambda: across(high_at, 0, 0))
                pl.when(has_low)(lambda: across(low_at, 2 * members, members))
            else:
                pl.when(has_high)(lambda: ended(high_at, 0))
                pl.when(has_low)(lambda: ended(low_at, members))
                for k in range(members):
                    pl.when((member == 0) & has_low)(lambda k=k: arrived(k, low_at))
                    pl.when((member == members - 1) & has_high)(
                        lambda k=k: arrived(2 * members + k, high_at)
                    )
        for a, margin in enumerate(margins):
            src, before, after = ins[a], outs[2 * a], outs[2 * a + 1]
            length = src.shape[0]
            to_right = remote(
                src.at[length - margin : length], before, send_halo.at[a, 0],
                recv_halo.at[a, 0], right_at,
            )
            to_left = remote(
                src.at[0:margin], after, send_halo.at[a, 1], recv_halo.at[a, 1], left_at
            )
            if action == "start":
                pl.when(has_right)(to_right.start)
                pl.when(has_left)(to_left.start)
            else:
                pl.when(has_right)(to_right.wait_send)
                pl.when(has_left)(to_left.wait_send)
                pl.when(has_left)(to_right.wait_recv)
                pl.when(has_right)(to_left.wait_recv)

    each("start")
    for a in range(shared):
        outs[2 * halos + a][members + member] = ins[halos + a][...]
    each("wait")


def exchange(halos, shared, number):
    members = lax.axis_size("dev")
    shapes = []
    for array, margin in halos:
        shapes += [jax.ShapeDtypeStruct((margin,) + array.shape[1:], array.dtype)] * 2
    for array in shared:
        shapes.append(jax.ShapeDtypeStruct((3 * members,) + array.shape, array.dtype))
    total = len(halos) + len(shared)
    vmem = pl.BlockSpec(memory_space=pltpu.VMEM)
    halo_count, share_count = max(len(halos), 1), max(len(shared), 1)
    return pl.pallas_call(
        functools.partial(exchange_kernel, [m for _, m in halos], len(shared)),
        out_shape=shapes,
        in_specs=[vmem] * total,
        out_specs=[vmem] * len(shapes),
        scratch_shapes=[
            pltpu.SemaphoreType.DMA((halo_count, 2)),
            pltpu.SemaphoreType.DMA((halo_count, 2)),
            pltpu.SemaphoreType.DMA((share_count, members + 1)),
            pltpu.SemaphoreType.DMA((share_count, 3 * members)),
        ],
        name=f"exchange_{number}",
        compiler_params=pltpu.CompilerParams(
            collective_id=number, has_side_effects=True, vmem_limit_bytes=LIMIT
        ),
    )(*[a for a, _ in halos], *shared)


def local(kernel, shapes, args, scalars, scratch):
    vmem = pl.BlockSpec(memory_space=pltpu.VMEM)
    smem = pl.BlockSpec(memory_space=pltpu.SMEM)
    return pl.pallas_call(
        kernel,
        out_shape=shapes,
        in_specs=[smem if i in scalars else vmem for i in range(len(args))],
        out_specs=[vmem] * len(shapes),
        scratch_shapes=scratch,
        name=kernel.__name__,
        compiler_params=pltpu.CompilerParams(vmem_limit_bytes=LIMIT),
    )(*args)


def conv_scratch(bricks, channels):
    width = 2 * channels
    return [
        pltpu.VMEM((bricks, SIDE, SIDE, SIDE, width), F32),
        pltpu.VMEM((3, PADDED, PADDED, SIDE, width), F32),
        pltpu.VMEM((VOX, 27 * width), BF16),
        pltpu.VMEM((width, 27 * width), BF16),
    ]


def per_device(
    x, fine_links, parent_codes, coarse_links,
    in_weight, in_bias, down, one_weight, one_bias, two_weight, two_bias, up, out_weight, out_bias,
):
    count, channels = x.shape[0], x.shape[1]
    slots, wide = coarse_links.shape[0], one_bias.shape[0]
    sized = lambda *shape: jax.ShapeDtypeStruct(shape, F32)
    row = lambda bias: bias.reshape(1, -1)
    code_block = jnp.pad(parent_codes.reshape(1, -1), ((0, 7), (0, 128 - count)))
    left, right, codes = exchange([(x, HALO)], [code_block], 1)
    codes = codes.reshape(-1, 128)
    hidden, pooled = local(
        first_kernel,
        [sized(count, VOX // 2, 2 * channels), sized(count, OCT // 2, 2 * channels)],
        [x, left, right, fine_links, in_weight, row(in_bias)],
        (3,),
        conv_scratch(count + 2 * HALO, channels),
    )
    hidden_left, hidden_right, pooled = exchange([(hidden, HALO)], [pooled], 2)
    (first,) = local(
        second_kernel,
        [sized(slots, VOX, wide)],
        [pooled, codes, coarse_links, down, one_weight, row(one_bias)],
        (1, 2),
        [pltpu.VMEM((3 * slots * 8, OCT, channels), F32)] + conv_scratch(3 * slots, wide),
    )
    first_left, first_right = exchange([(first, slots)], [], 3)
    (lifted,) = local(
        third_kernel,
        [sized(slots * 8, OCT // 2, 2 * channels)],
        [first, first_left, first_right, coarse_links, two_weight, row(two_bias), up],
        (3,),
        conv_scratch(3 * slots, wide),
    )
    (lifted,) = exchange([], [lifted], 4)
    (out,) = local(
        fourth_kernel,
        [sized(count, channels, VOX)],
        [x, hidden, hidden_left, hidden_right, lifted, codes, fine_links, out_weight, row(out_bias)],
        (5, 6),
        conv_scratch(count + 2 * HALO, channels),
    )
    return out


def solution(mesh):
    bricks = P(("grp", "dev"), None, None)
    rows = P(("grp", "dev"), None)
    placed = (bricks, rows, P(("grp", "dev")), rows) + (P(),) * 10
    return jax.shard_map(
        per_device, mesh=mesh, in_specs=placed, out_specs=bricks, check_vma=False
    )
```

```python
import functools

import jax
import jax.numpy as jnp
from jax import lax
from jax.experimental import pallas as pl
from jax.experimental.pallas import tpu as pltpu
from jax.sharding import PartitionSpec as P

F32 = jnp.float32
BF16 = jnp.bfloat16
MESH = pl.DeviceIdType.MESH
SIDE = 8
VOX = SIDE * SIDE * SIDE
OCT = VOX // 8
PADDED = SIDE + 2
HALO = 2
FINE_ROWS = 304
COARSE_ROWS = 296
LIMIT = 60 * 1024 * 1024

offsets = [(x, y, z) for x in (-1, 0, 1) for y in (-1, 0, 1) for z in (-1, 0, 1)]
columns = {o: k for k, o in enumerate(o for o in offsets if o != (0, 0, 0))}
source = {-1: slice(7, 8), 0: slice(0, 8), 1: slice(0, 1)}
target = {-1: slice(0, 1), 0: slice(1, 9), 1: slice(9, 10)}


def split(v):
    high = v.astype(BF16).astype(F32)
    return high, v - high


def silu(v):
    return v / (1.0 + jnp.exp(-v))


def product(a, b, dims=((1,), (1,))):
    return lax.dot_general(a, b, (dims, ((), ())), preferred_element_type=F32)


def precise(a, b, dims=((1,), (1,))):
    return lax.dot_general(
        a, b, (dims, ((), ())), preferred_element_type=F32, precision=lax.Precision.HIGHEST
    )


def spread(v):
    half = v.shape[0] // 2
    return jnp.concatenate([v[:half], v[half:]], axis=1)


def unspread(v):
    width = v.shape[1] // 2
    return jnp.concatenate([v[:, :width], v[:, width:]], axis=0)


def surface_rank(p):
    x, y, z = p // 64, p // 8 % 8, p % 8
    inner = jnp.where(z == 0, 0, jnp.where(z == 7, 1, -1))
    inner = jnp.where(inner < 0, -1, 224 + ((x - 1) * 6 + y - 1) * 2 + inner)
    side = 128 + (x - 1) * 16 + z
    edge = jnp.where(y == 0, side, jnp.where(y == 7, side + 8, inner))
    return jnp.where(x == 0, p, jnp.where(x == 7, p - 384, edge))


def surface_pick(rows):
    rank = surface_rank(lax.broadcasted_iota(jnp.int32, (1, VOX), 1))
    row = lax.broadcasted_iota(jnp.int32, (rows, VOX), 0)
    return jnp.where(row == rank, 1.0, 0.0).astype(BF16)


def surface_place(rows):
    rank = surface_rank(lax.broadcasted_iota(jnp.int32, (VOX, rows), 0))
    col = lax.broadcasted_iota(jnp.int32, (VOX, rows), 1)
    return jnp.where(col == rank, 1.0, 0.0).astype(BF16)


def both_parts(v):
    high, low = split(v)
    return jnp.concatenate([high, low], axis=1).astype(BF16)


def joined(sums):
    width = sums.shape[1] // 2
    return sums[:, :width] + sums[:, width:]


def put_surface(parts, index, placing, v):
    sums = product(placing, both_parts(v), ((1,), (0,)))
    parts[index] = sums.reshape(SIDE, SIDE, SIDE, sums.shape[1])


def put_parts(parts, index, v):
    high, low = split(v)
    parts[index] = jnp.concatenate([high, low], axis=1).reshape(SIDE, SIDE, SIDE, 2 * v.shape[1])


def fill(parts, own, start, links, brick, padded):
    for dx, dy, dz in offsets:
        spot = (dz + 1, target[dx], target[dy])
        if (dx, dy, dz) == (0, 0, 0):
            padded[spot] = parts[own]
            continue
        link = links[brick, columns[dx, dy, dz]]
        found = link >= 0
        row = jnp.where(found, link - start, own)
        keep = jnp.where(found, 1.0, 0.0).astype(F32)
        padded[spot] = parts[row, source[dx], source[dy]] * keep


def unfold(padded, patches):
    width = padded.shape[-1]
    z_at = lax.broadcasted_iota(jnp.int32, (PADDED, SIDE, width), 1)
    for x in range(PADDED):
        middle = padded[1, x]
        padded[0, x] = pltpu.roll(jnp.where(z_at == SIDE - 1, padded[0, x], middle), 1, 1)
        padded[2, x] = pltpu.roll(jnp.where(z_at == 0, padded[2, x], middle), SIDE - 1, 1)
    for i in range(3):
        for j in range(3):
            for k in range(3):
                tap = 9 * i + 3 * j + k
                window = padded[k, i : i + SIDE, j : j + SIDE].reshape(VOX, width)
                patches[:, tap * width : (tap + 1) * width] = window.astype(BF16)


def fine_matrix(weight, matrix):
    channels = weight.shape[0]
    lane = lax.broadcasted_iota(jnp.int32, (channels, 2 * channels), 1)
    for pair in range(14):
        if pair < 13:
            tile = weight[:, pair * 2 * channels : (pair + 1) * 2 * channels]
            turned = pltpu.roll(tile, channels, 1)
            taps = [
                jnp.where(lane < channels, tile, turned),
                jnp.where(lane < channels, turned, tile),
            ]
        else:
            tile = weight[:, 26 * channels : 27 * channels]
            taps = [jnp.concatenate([tile, tile], axis=1)]
        for at, tap in enumerate(taps):
            high, low = split(tap)
            cols = slice((2 * pair + at) * 2 * channels, (2 * pair + at + 1) * 2 * channels)
            matrix[0:channels, cols] = high.astype(BF16)
            matrix[channels : 2 * channels, cols] = low.astype(BF16)


def coarse_matrix(weight, matrix):
    channels = weight.shape[0]
    for tap in range(27):
        high, low = split(weight[:, tap * channels : (tap + 1) * channels])
        for part in range(2):
            cols = slice((2 * tap + part) * channels, (2 * tap + part + 1) * channels)
            matrix[0:channels, cols] = high.astype(BF16)
            matrix[channels : 2 * channels, cols] = low.astype(BF16)


def convolved(parts, own, start, links, brick, padded, patches, matrix, bias):
    fill(parts, own, start, links, brick, padded)
    unfold(padded, patches)
    both = product(patches[...], matrix[...])
    channels = both.shape[1] // 2
    return both[:, :channels] + both[:, channels:] + bias[...]


def place():
    return lax.axis_index("grp"), lax.axis_index("dev"), lax.axis_size("grp"), lax.axis_size("dev")


def pack_kernel(x, packed):
    pick = surface_pick(FINE_ROWS)
    for i in range(x.shape[0]):
        high, low = split(x[i])
        packed[i] = spread(product(pick, high.astype(BF16)) + product(pick, low.astype(BF16)))


def first_kernel(x, left, right, links, weight, bias, hidden, packed, pooled, parts, padded, patches, matrix):
    group, member, _, members = place()
    count = x.shape[0]
    start = (group * members + member) * count - HALO
    for i in range(count):
        put_parts(parts, HALO + i, x[i].T)
    placing = surface_place(FINE_ROWS)
    for i in range(HALO):
        put_surface(parts, i, placing, unspread(left[i]))
        put_surface(parts, HALO + count + i, placing, unspread(right[i]))
    pick = surface_pick(FINE_ROWS)
    fine_matrix(weight, matrix)
    row = lax.broadcasted_iota(jnp.int32, (OCT, VOX), 0)
    col = lax.broadcasted_iota(jnp.int32, (OCT, VOX), 1)
    cell = (col // 128) * 16 + (col // 16 % 4) * 4 + col // 2 % 4
    pooling = jnp.where(row == cell, 0.125, 0.0).astype(BF16)

    def step(i, carry):
        out = silu(
            convolved(parts, HALO + i, start, links, i, padded, patches, matrix, bias)
        )
        hidden[i] = spread(out)
        both = both_parts(out)
        pooled[i] = spread(joined(product(pooling, both, ((1,), (0,)))))
        packed[i] = spread(joined(product(pick, both, ((1,), (0,)))))
        return carry

    lax.fori_loop(0, count, step, 0)


def octant_order(flip):
    row = lax.broadcasted_iota(jnp.int32, (VOX, VOX), 1 if flip else 0)
    col = lax.broadcasted_iota(jnp.int32, (VOX, VOX), 0 if flip else 1)
    x, y, z = row // 64, row // 8 % 8, row % 8
    spot = (x // 4 * 4 + y // 4 * 2 + z // 4) * 64 + x % 4 * 16 + y % 4 * 4 + z % 4
    return jnp.where(spot == col, 1.0, 0.0).astype(BF16)


def second_kernel(pooled, codes, links, down, weight, bias, first, packed, pieces, parts, padded, patches, matrix):
    group, member, groups, members = place()
    slots = links.shape[0]
    count = pooled.shape[1]
    start = (group * members + member - 1) * slots
    position = group * members + member
    pieces[...] = jnp.zeros_like(pieces)
    coarse_matrix(weight, matrix)
    for near in range(3):
        there = position + near - 1
        there_group = (there + members) // members - 1
        there_member = there - there_group * members
        band = there_group - group + 1
        valid = (there >= 0) & (there < groups * members)
        for one in range(count):

            def visit(owner, carry):
                code = codes[(band * members + owner) * 8, one] - there_member * slots * 8

                @pl.when(valid & (code >= 0) & (code < slots * 8))
                def _():
                    pieces[near * slots * 8 + code] = unspread(
                        pooled[band * members + owner, one]
                    )

                return carry

            lax.fori_loop(0, members, visit, 0)
    order = octant_order(False)

    def base(slot, carry):
        piece = pieces[pl.ds(slot * 8, 8)].reshape(VOX, pieces.shape[-1])
        lifted = precise(piece, down[...])
        high, low = split(lifted)
        both = jnp.concatenate([high, low], axis=1).astype(BF16)
        parts[slot] = product(order, both, ((1,), (0,))).reshape(SIDE, SIDE, SIDE, both.shape[1])
        return carry

    lax.fori_loop(0, 3 * slots, base, 0)
    pick = surface_pick(COARSE_ROWS)

    def step(i, carry):
        out = silu(
            convolved(parts, slots + i, start, links, i, padded, patches, matrix, bias)
        )
        first[i] = out
        packed[i] = joined(product(pick, both_parts(out), ((1,), (0,))))
        return carry

    lax.fori_loop(0, slots, step, 0)


def third_kernel(first, left, right, links, codes, weight, bias, up, wanted, lifted, parts, padded, patches, matrix):
    group, member, _, members = place()
    slots = links.shape[0]
    start = (group * members + member - 1) * slots
    coarse_matrix(weight, matrix)
    placing = surface_place(COARSE_ROWS)
    for i in range(slots):
        put_surface(parts, i, placing, left[i])
        put_parts(parts, slots + i, first[i])
        put_surface(parts, 2 * slots + i, placing, right[i])
    order = octant_order(True)

    def step(i, carry):
        out = silu(
            convolved(parts, slots + i, start, links, i, padded, patches, matrix, bias)
        )
        high, low = split(precise(out, up[...]))
        both = jnp.concatenate([high, low], axis=1).astype(BF16)
        sums = product(order, both, ((1,), (0,)))
        width = high.shape[1]
        ordered = sums[:, :width] + sums[:, width:]
        for octant in range(8):
            lifted[i * 8 + octant] = spread(ordered[octant * OCT : (octant + 1) * OCT])
        return carry

    lax.fori_loop(0, slots, step, 0)
    bricks = wanted.shape[0] - 2 * HALO
    each = bricks // members
    zeros = jnp.zeros((HALO,) + wanted.shape[1:], F32)
    wanted[0:HALO] = zeros
    wanted[HALO + bricks :] = zeros

    def choose(j, carry):
        code = codes[(members + j // each) * 8, j % each] - member * slots * 8
        mine = (code >= 0) & (code < slots * 8)
        keep = jnp.where(mine, 1.0, 0.0).astype(F32)
        wanted[HALO + j] = lifted[jnp.where(mine, code, 0)] * keep
        return carry

    lax.fori_loop(0, bricks, choose, 0)


def fourth_kernel(x, hidden, left, right, window, low, high, links, weight, bias, out, parts, padded, patches, matrix):
    group, member, groups, members = place()
    count = x.shape[0]
    start = (group * members + member) * count - HALO
    fine_matrix(weight, matrix)
    row = lax.broadcasted_iota(jnp.int32, (VOX, OCT), 0)
    col = lax.broadcasted_iota(jnp.int32, (VOX, OCT), 1)
    cell = (row // 128) * 16 + (row // 16 % 4) * 4 + row // 2 % 4
    repeat = jnp.where(col == cell, 1.0, 0.0).astype(BF16)
    placing = surface_place(FINE_ROWS)
    for i in range(count + 2 * HALO):
        piece = window[0, i]
        for owner in range(1, members):
            piece = piece + window[owner, i]
        if i < HALO:
            other = low[0, i]
            for owner in range(1, members):
                other = other + low[owner, i]
            piece = jnp.where(member == 0, other, piece)
        elif i >= HALO + count:
            other = high[0, i - HALO - count]
            for owner in range(1, members):
                other = other + high[owner, i - HALO - count]
            piece = jnp.where(member == members - 1, other, piece)
        rising = joined(product(repeat, both_parts(unspread(piece)), ((1,), (0,))))
        if i < HALO:
            held = joined(
                product(placing, both_parts(unspread(left[i])), ((1,), (0,)))
            )
        elif i < HALO + count:
            held = unspread(hidden[i - HALO])
        else:
            held = joined(
                product(placing, both_parts(unspread(right[i - HALO - count])), ((1,), (0,)))
            )
        put_parts(parts, i, silu(held + rising))

    def step(i, carry):
        conv = convolved(parts, HALO + i, start, links, i, padded, patches, matrix, bias)
        out[i] = x[i] + conv.T
        return carry

    lax.fori_loop(0, count, step, 0)


def exchange_kernel(margins, shared, windows, *refs):
    halos = len(margins)
    total = halos + shared + windows
    given = 2 * halos + shared + 3 * windows
    ins, outs = refs[:total], refs[total : total + given]
    send_halo, recv_halo, send_all, recv_all = refs[total + given :]
    group, member, groups, members = place()
    position = group * members + member
    whole = groups * members
    has_left, has_right = position > 0, position < whole - 1
    has_low, has_high = group > 0, group < groups - 1
    left_at = (jnp.maximum(position - 1, 0) // members, (position + members - 1) % members)
    right_at = (jnp.minimum(position + 1, whole - 1) // members, (position + 1) % members)
    low_at = (jnp.maximum(group - 1, 0), members - 1)
    high_at = (jnp.minimum(group + 1, groups - 1), 0)

    barrier = pltpu.get_barrier_semaphore()

    def greet(where):
        pl.semaphore_signal(barrier, inc=1, device_id=where, device_id_type=MESH)

    count = jnp.int32(0)
    if halos:
        pl.when(has_left)(lambda: greet(left_at))
        pl.when(has_right)(lambda: greet(right_at))
        count = count + jnp.where(has_left, 1, 0) + jnp.where(has_right, 1, 0)
    if shared or windows:
        for k in range(1, members):
            greet((group, (member + k) % members))
        for k in range(members):
            pl.when((member == 0) & has_low)(lambda k=k: greet((low_at[0], k)))
            pl.when((member == members - 1) & has_high)(lambda k=k: greet((high_at[0], k)))
        count = count + (members - 1) + jnp.where(has_low, 1, 0) + jnp.where(has_high, 1, 0)
    pl.semaphore_wait(barrier, count)

    def remote(src, dst, send, recv, where):
        return pltpu.make_async_remote_copy(
            src_ref=src, dst_ref=dst, send_sem=send, recv_sem=recv,
            device_id=where, device_id_type=MESH,
        )

    def parts_of(a):
        src = ins[halos + a]
        if a < shared:
            out = outs[2 * halos + a]
            return (
                lambda to: src, src, src,
                lambda by: out.at[members + by],
                lambda by: out.at[by],
                lambda by: out.at[2 * members + by],
            )
        window, low, high = outs[2 * halos + shared + 3 * (a - shared) :][:3]
        span = window.shape[1]
        each = span - 2 * HALO
        bricks = src.shape[0] - 2 * HALO
        return (
            lambda to: src.at[pl.ds(to * each, span)],
            src.at[bricks : bricks + HALO],
            src.at[HALO : 2 * HALO],
            lambda by: window.at[by],
            lambda by: low.at[by],
            lambda by: high.at[by],
        )

    def each(action):
        for a in range(shared + windows):
            own, up, down, here, below, above = parts_of(a)
            sends, recvs = send_all.at[a], recv_all.at[a]
            for k in range(1, members):
                other = (member + k) % members
                by = member if action == "start" else other
                copy = remote(
                    own(other), here(by), sends.at[k], recvs.at[members + by], (group, other)
                )
                copy.start() if action == "start" else copy.wait()
            to_high = remote(up, below(member), sends.at[0], recvs.at[member], high_at)
            to_low = remote(
                down, above(member), sends.at[members], recvs.at[2 * members + member], low_at
            )
            if action == "start":
                pl.when(has_high)(to_high.start)
                pl.when(has_low)(to_low.start)
            else:
                pl.when(has_high)(to_high.wait_send)
                pl.when(has_low)(to_low.wait_send)
                for k in range(members):
                    from_low = remote(up, below(k), sends.at[0], recvs.at[k], low_at)
                    from_high = remote(
                        down, above(k), sends.at[0], recvs.at[2 * members + k], high_at
                    )
                    pl.when((member == 0) & has_low)(from_low.wait_recv)
                    pl.when((member == members - 1) & has_high)(from_high.wait_recv)
        for a, margin in enumerate(margins):
            src, before, after = ins[a], outs[2 * a], outs[2 * a + 1]
            length = src.shape[0]
            to_right = remote(
                src.at[length - margin : length], before, send_halo.at[a, 0],
                recv_halo.at[a, 0], right_at,
            )
            to_left = remote(
                src.at[0:margin], after, send_halo.at[a, 1], recv_halo.at[a, 1], left_at
            )
            if action == "start":
                pl.when(has_right)(to_right.start)
                pl.when(has_left)(to_left.start)
            else:
                pl.when(has_right)(to_right.wait_send)
                pl.when(has_left)(to_left.wait_send)
                pl.when(has_left)(to_right.wait_recv)
                pl.when(has_right)(to_left.wait_recv)

    each("start")
    for a in range(shared):
        outs[2 * halos + a][members + member] = ins[halos + a][...]
    for a in range(shared, shared + windows):
        window, src = outs[2 * halos + shared + 3 * (a - shared)], ins[halos + a]
        span = window.shape[1]
        window[member] = src[pl.ds(member * (span - 2 * HALO), span)]
    each("wait")


def exchange(halos, shared, windows, number):
    members = lax.axis_size("dev")
    shapes = []
    for array, margin in halos:
        shapes += [jax.ShapeDtypeStruct((margin,) + array.shape[1:], array.dtype)] * 2
    for array in shared:
        shapes.append(jax.ShapeDtypeStruct((3 * members,) + array.shape, array.dtype))
    for array in windows:
        span = (array.shape[0] - 2 * HALO) // members + 2 * HALO
        for rows in (span, HALO, HALO):
            shapes.append(
                jax.ShapeDtypeStruct((members, rows) + array.shape[1:], array.dtype)
            )
    total = len(halos) + len(shared) + len(windows)
    vmem = pl.BlockSpec(memory_space=pltpu.VMEM)
    halo_count, share_count = max(len(halos), 1), max(len(shared) + len(windows), 1)
    return pl.pallas_call(
        functools.partial(exchange_kernel, [m for _, m in halos], len(shared), len(windows)),
        out_shape=shapes,
        in_specs=[vmem] * total,
        out_specs=[vmem] * len(shapes),
        scratch_shapes=[
            pltpu.SemaphoreType.DMA((halo_count, 2)),
            pltpu.SemaphoreType.DMA((halo_count, 2)),
            pltpu.SemaphoreType.DMA((share_count, members + 1)),
            pltpu.SemaphoreType.DMA((share_count, 3 * members)),
        ],
        name=f"exchange_{number}",
        compiler_params=pltpu.CompilerParams(
            collective_id=number, has_side_effects=True, vmem_limit_bytes=LIMIT
        ),
    )(*[a for a, _ in halos], *shared, *windows)


def local(kernel, shapes, args, scalars, scratch):
    vmem = pl.BlockSpec(memory_space=pltpu.VMEM)
    smem = pl.BlockSpec(memory_space=pltpu.SMEM)
    return pl.pallas_call(
        kernel,
        out_shape=shapes,
        in_specs=[smem if i in scalars else vmem for i in range(len(args))],
        out_specs=[vmem] * len(shapes),
        scratch_shapes=scratch,
        name=kernel.__name__,
        compiler_params=pltpu.CompilerParams(vmem_limit_bytes=LIMIT),
    )(*args)


def conv_scratch(bricks, channels):
    width = 2 * channels
    return [
        pltpu.VMEM((bricks, SIDE, SIDE, SIDE, width), F32),
        pltpu.VMEM((3, PADDED, PADDED, SIDE, width), F32),
        pltpu.VMEM((VOX, 27 * width), BF16),
        pltpu.VMEM((width, 27 * width), BF16),
    ]


def per_device(
    x, fine_links, parent_codes, coarse_links,
    in_weight, in_bias, down, one_weight, one_bias, two_weight, two_bias, up, out_weight, out_bias,
):
    count, channels = x.shape[0], x.shape[1]
    slots, wide = coarse_links.shape[0], one_bias.shape[0]
    sized = lambda *shape: jax.ShapeDtypeStruct(shape, F32)
    row = lambda bias: bias.reshape(1, -1)
    code_block = jnp.pad(parent_codes.reshape(1, -1), ((0, 7), (0, 128 - count)))
    members = lax.axis_size("dev")
    flat = (FINE_ROWS // 2, 2 * channels)
    (packed,) = local(pack_kernel, [sized(count, *flat)], [x], (), [])
    left, right, codes = exchange([(packed, HALO)], [code_block], [], 1)
    codes = codes.reshape(-1, 128)
    hidden, packed, pooled = local(
        first_kernel,
        [
            sized(count, VOX // 2, 2 * channels),
            sized(count, *flat),
            sized(count, OCT // 2, 2 * channels),
        ],
        [x, left, right, fine_links, in_weight, row(in_bias)],
        (3,),
        conv_scratch(count + 2 * HALO, channels),
    )
    hidden_left, hidden_right, pooled = exchange([(packed, HALO)], [pooled], [], 2)
    first, packed = local(
        second_kernel,
        [sized(slots, VOX, wide), sized(slots, COARSE_ROWS, wide)],
        [pooled, codes, coarse_links, down, one_weight, row(one_bias)],
        (1, 2),
        [pltpu.VMEM((3 * slots * 8, OCT, channels), F32)] + conv_scratch(3 * slots, wide),
    )
    first_left, first_right = exchange([(packed, slots)], [], [], 3)
    (wanted,) = local(
        third_kernel,
        [sized(members * count + 2 * HALO, OCT // 2, 2 * channels)],
        [first, first_left, first_right, coarse_links, codes, two_weight, row(two_bias), up],
        (3, 4),
        [pltpu.VMEM((slots * 8, OCT // 2, 2 * channels), F32)] + conv_scratch(3 * slots, wide),
    )
    window, low, high = exchange([], [], [wanted], 4)
    (out,) = local(
        fourth_kernel,
        [sized(count, channels, VOX)],
        [x, hidden, hidden_left, hidden_right, window, low, high, fine_links, out_weight,
         row(out_bias)],
        (7,),
        conv_scratch(count + 2 * HALO, channels),
    )
    return out


def solution(mesh):
    bricks = P(("grp", "dev"), None, None)
    rows = P(("grp", "dev"), None)
    placed = (bricks, rows, P(("grp", "dev")), rows) + (P(),) * 10
    return jax.shard_map(
        per_device, mesh=mesh, in_specs=placed, out_specs=bricks, check_vma=False
    )
```

```python
import functools

import jax
import jax.numpy as jnp
from jax import lax
from jax.experimental import pallas as pl
from jax.experimental.pallas import tpu as pltpu
from jax.sharding import PartitionSpec as P

F32 = jnp.float32
BF16 = jnp.bfloat16
MESH = pl.DeviceIdType.MESH
SIDE = 8
VOX = SIDE * SIDE * SIDE
OCT = VOX // 8
PADDED = SIDE + 2
HALO = 2
FINE_ROWS = 304
COARSE_ROWS = 296
LIMIT = 60 * 1024 * 1024

offsets = [(x, y, z) for x in (-1, 0, 1) for y in (-1, 0, 1) for z in (-1, 0, 1)]
columns = {o: k for k, o in enumerate(o for o in offsets if o != (0, 0, 0))}
source = {-1: slice(7, 8), 0: slice(0, 8), 1: slice(0, 1)}
target = {-1: slice(0, 1), 0: slice(1, 9), 1: slice(9, 10)}


def split(v):
    high = v.astype(BF16).astype(F32)
    return high, v - high


def silu(v):
    return v / (1.0 + jnp.exp(-v))


def product(a, b, dims=((1,), (1,))):
    return lax.dot_general(a, b, (dims, ((), ())), preferred_element_type=F32)


def precise(a, b, dims=((1,), (1,))):
    (a_high, a_low), (b_high, b_low) = split(a), split(b)
    a_high, a_low, b_high, b_low = (v.astype(BF16) for v in (a_high, a_low, b_high, b_low))
    return product(a_high, b_high, dims) + product(a_low, b_high, dims) + product(a_high, b_low, dims)


def spread(v):
    half = v.shape[0] // 2
    return jnp.concatenate([v[:half], v[half:]], axis=1)


def unspread(v):
    width = v.shape[1] // 2
    return jnp.concatenate([v[:, :width], v[:, width:]], axis=0)


def surface_rank(p):
    x, y, z = p // 64, p // 8 % 8, p % 8
    inner = jnp.where(z == 0, 0, jnp.where(z == 7, 1, -1))
    inner = jnp.where(inner < 0, -1, 224 + ((x - 1) * 6 + y - 1) * 2 + inner)
    side = 128 + (x - 1) * 16 + z
    edge = jnp.where(y == 0, side, jnp.where(y == 7, side + 8, inner))
    return jnp.where(x == 0, p, jnp.where(x == 7, p - 384, edge))


def surface_pick(rows):
    rank = surface_rank(lax.broadcasted_iota(jnp.int32, (1, VOX), 1))
    row = lax.broadcasted_iota(jnp.int32, (rows, VOX), 0)
    return jnp.where(row == rank, 1.0, 0.0).astype(BF16)


def surface_place(rows):
    rank = surface_rank(lax.broadcasted_iota(jnp.int32, (VOX, rows), 0))
    col = lax.broadcasted_iota(jnp.int32, (VOX, rows), 1)
    return jnp.where(col == rank, 1.0, 0.0).astype(BF16)


def both_parts(v):
    high, low = split(v)
    return jnp.concatenate([high, low], axis=1).astype(BF16)


def joined(sums):
    width = sums.shape[1] // 2
    return sums[:, :width] + sums[:, width:]


def put_surface(parts, index, placing, v):
    sums = product(placing, both_parts(v), ((1,), (0,)))
    parts[index] = sums.reshape(SIDE, SIDE, SIDE, sums.shape[1])


def put_parts(parts, index, v):
    high, low = split(v)
    parts[index] = jnp.concatenate([high, low], axis=1).reshape(SIDE, SIDE, SIDE, 2 * v.shape[1])


def fill(parts, own, start, links, brick, padded):
    for dx, dy, dz in offsets:
        spot = (dz + 1, target[dx], target[dy])
        if (dx, dy, dz) == (0, 0, 0):
            padded[spot] = parts[own]
            continue
        link = links[brick, columns[dx, dy, dz]]
        found = link >= 0
        row = jnp.where(found, link - start, own)
        keep = jnp.where(found, 1.0, 0.0).astype(F32)
        padded[spot] = parts[row, source[dx], source[dy]] * keep


def unfold(padded, patches):
    width = padded.shape[-1]
    z_at = lax.broadcasted_iota(jnp.int32, (PADDED, SIDE, width), 1)
    for x in range(PADDED):
        middle = padded[1, x]
        padded[0, x] = pltpu.roll(jnp.where(z_at == SIDE - 1, padded[0, x], middle), 1, 1)
        padded[2, x] = pltpu.roll(jnp.where(z_at == 0, padded[2, x], middle), SIDE - 1, 1)
    for i in range(3):
        for j in range(3):
            for k in range(3):
                tap = 9 * i + 3 * j + k
                window = padded[k, i : i + SIDE, j : j + SIDE].reshape(VOX, width)
                patches[:, tap * width : (tap + 1) * width] = window.astype(BF16)


def fine_matrix(weight, matrix):
    channels = weight.shape[0]
    lane = lax.broadcasted_iota(jnp.int32, (channels, 2 * channels), 1)
    for pair in range(14):
        if pair < 13:
            tile = weight[:, pair * 2 * channels : (pair + 1) * 2 * channels]
            turned = pltpu.roll(tile, channels, 1)
            taps = [
                jnp.where(lane < channels, tile, turned),
                jnp.where(lane < channels, turned, tile),
            ]
        else:
            tile = weight[:, 26 * channels : 27 * channels]
            taps = [jnp.concatenate([tile, tile], axis=1)]
        for at, tap in enumerate(taps):
            high, low = split(tap)
            cols = slice((2 * pair + at) * 2 * channels, (2 * pair + at + 1) * 2 * channels)
            matrix[0:channels, cols] = high.astype(BF16)
            matrix[channels : 2 * channels, cols] = low.astype(BF16)


def coarse_matrix(weight, matrix):
    channels = weight.shape[0]
    for tap in range(27):
        high, low = split(weight[:, tap * channels : (tap + 1) * channels])
        for part in range(2):
            cols = slice((2 * tap + part) * channels, (2 * tap + part + 1) * channels)
            matrix[0:channels, cols] = high.astype(BF16)
            matrix[channels : 2 * channels, cols] = low.astype(BF16)


def convolved(parts, own, start, links, brick, padded, patches, matrix, bias):
    fill(parts, own, start, links, brick, padded)
    unfold(padded, patches)
    both = product(patches[...], matrix[...])
    channels = both.shape[1] // 2
    return both[:, :channels] + both[:, channels:] + bias[...]


def place():
    return lax.axis_index("grp"), lax.axis_index("dev"), lax.axis_size("grp"), lax.axis_size("dev")


def pack_kernel(x, packed):
    pick = surface_pick(FINE_ROWS)
    for i in range(x.shape[0]):
        high, low = split(x[i])
        packed[i] = spread(product(pick, high.astype(BF16)) + product(pick, low.astype(BF16)))


def first_kernel(x, left, right, links, weight, bias, hidden, packed, pooled, parts, padded, patches, matrix):
    group, member, _, members = place()
    count = x.shape[0]
    start = (group * members + member) * count - HALO
    for i in range(count):
        put_parts(parts, HALO + i, x[i].T)
    placing = surface_place(FINE_ROWS)
    for i in range(HALO):
        put_surface(parts, i, placing, unspread(left[i]))
        put_surface(parts, HALO + count + i, placing, unspread(right[i]))
    pick = surface_pick(FINE_ROWS)
    fine_matrix(weight, matrix)
    row = lax.broadcasted_iota(jnp.int32, (OCT, VOX), 0)
    col = lax.broadcasted_iota(jnp.int32, (OCT, VOX), 1)
    cell = (col // 128) * 16 + (col // 16 % 4) * 4 + col // 2 % 4
    pooling = jnp.where(row == cell, 0.125, 0.0).astype(BF16)

    def step(i, carry):
        out = silu(
            convolved(parts, HALO + i, start, links, i, padded, patches, matrix, bias)
        )
        hidden[i] = spread(out)
        both = both_parts(out)
        pooled[i] = spread(joined(product(pooling, both, ((1,), (0,)))))
        packed[i] = spread(joined(product(pick, both, ((1,), (0,)))))
        return carry

    lax.fori_loop(0, count, step, 0)


def octant_order(flip):
    row = lax.broadcasted_iota(jnp.int32, (VOX, VOX), 1 if flip else 0)
    col = lax.broadcasted_iota(jnp.int32, (VOX, VOX), 0 if flip else 1)
    x, y, z = row // 64, row // 8 % 8, row % 8
    spot = (x // 4 * 4 + y // 4 * 2 + z // 4) * 64 + x % 4 * 16 + y % 4 * 4 + z % 4
    return jnp.where(spot == col, 1.0, 0.0).astype(BF16)


def second_kernel(pooled, codes, links, down, weight, bias, first, packed, pieces, parts, padded, patches, matrix):
    group, member, groups, members = place()
    slots = links.shape[0]
    count = pooled.shape[1]
    start = (group * members + member - 1) * slots
    position = group * members + member
    pieces[...] = jnp.zeros_like(pieces)
    coarse_matrix(weight, matrix)
    for near in range(3):
        there = position + near - 1
        there_group = (there + members) // members - 1
        there_member = there - there_group * members
        band = there_group - group + 1
        valid = (there >= 0) & (there < groups * members)
        for one in range(count):

            def visit(owner, carry):
                code = codes[(band * members + owner) * 8, one] - there_member * slots * 8

                @pl.when(valid & (code >= 0) & (code < slots * 8))
                def _():
                    pieces[near * slots * 8 + code] = unspread(
                        pooled[band * members + owner, one]
                    )

                return carry

            lax.fori_loop(0, members, visit, 0)
    order = octant_order(False)

    def base(slot, carry):
        piece = pieces[pl.ds(slot * 8, 8)].reshape(VOX, pieces.shape[-1])
        lifted = precise(piece, down[...], ((1,), (0,)))
        high, low = split(lifted)
        both = jnp.concatenate([high, low], axis=1).astype(BF16)
        parts[slot] = product(order, both, ((1,), (0,))).reshape(SIDE, SIDE, SIDE, both.shape[1])
        return carry

    lax.fori_loop(0, 3 * slots, base, 0)
    pick = surface_pick(COARSE_ROWS)

    def step(i, carry):
        out = silu(
            convolved(parts, slots + i, start, links, i, padded, patches, matrix, bias)
        )
        first[i] = out
        packed[i] = joined(product(pick, both_parts(out), ((1,), (0,))))
        return carry

    lax.fori_loop(0, slots, step, 0)


def third_kernel(first, left, right, links, codes, weight, bias, up, wanted, lifted, parts, padded, patches, matrix):
    group, member, _, members = place()
    slots = links.shape[0]
    start = (group * members + member - 1) * slots
    coarse_matrix(weight, matrix)
    placing = surface_place(COARSE_ROWS)
    for i in range(slots):
        put_surface(parts, i, placing, left[i])
        put_parts(parts, slots + i, first[i])
        put_surface(parts, 2 * slots + i, placing, right[i])
    order = octant_order(True)

    def step(i, carry):
        out = silu(
            convolved(parts, slots + i, start, links, i, padded, patches, matrix, bias)
        )
        high, low = split(precise(out, up[...]))
        both = jnp.concatenate([high, low], axis=1).astype(BF16)
        sums = product(order, both, ((1,), (0,)))
        width = high.shape[1]
        ordered = sums[:, :width] + sums[:, width:]
        for octant in range(8):
            lifted[i * 8 + octant] = spread(ordered[octant * OCT : (octant + 1) * OCT])
        return carry

    lax.fori_loop(0, slots, step, 0)
    bricks = wanted.shape[0] - 2 * HALO
    each = bricks // members
    zeros = jnp.zeros((HALO,) + wanted.shape[1:], F32)
    wanted[0:HALO] = zeros
    wanted[HALO + bricks :] = zeros

    def choose(j, carry):
        code = codes[(members + j // each) * 8, j % each] - member * slots * 8
        mine = (code >= 0) & (code < slots * 8)
        keep = jnp.where(mine, 1.0, 0.0).astype(F32)
        wanted[HALO + j] = lifted[jnp.where(mine, code, 0)] * keep
        return carry

    lax.fori_loop(0, bricks, choose, 0)


def fourth_kernel(x, hidden, left, right, window, low, high, links, weight, bias, out, parts, padded, patches, matrix):
    group, member, groups, members = place()
    count = x.shape[0]
    start = (group * members + member) * count - HALO
    fine_matrix(weight, matrix)
    row = lax.broadcasted_iota(jnp.int32, (VOX, OCT), 0)
    col = lax.broadcasted_iota(jnp.int32, (VOX, OCT), 1)
    cell = (row // 128) * 16 + (row // 16 % 4) * 4 + row // 2 % 4
    repeat = jnp.where(col == cell, 1.0, 0.0).astype(BF16)
    placing = surface_place(FINE_ROWS)
    for i in range(count + 2 * HALO):
        piece = window[0, i]
        for owner in range(1, members):
            piece = piece + window[owner, i]
        if i < HALO:
            other = low[0, i]
            for owner in range(1, members):
                other = other + low[owner, i]
            piece = jnp.where(member == 0, other, piece)
        elif i >= HALO + count:
            other = high[0, i - HALO - count]
            for owner in range(1, members):
                other = other + high[owner, i - HALO - count]
            piece = jnp.where(member == members - 1, other, piece)
        rising = joined(product(repeat, both_parts(unspread(piece)), ((1,), (0,))))
        if i < HALO:
            held = joined(
                product(placing, both_parts(unspread(left[i])), ((1,), (0,)))
            )
        elif i < HALO + count:
            held = unspread(hidden[i - HALO])
        else:
            held = joined(
                product(placing, both_parts(unspread(right[i - HALO - count])), ((1,), (0,)))
            )
        put_parts(parts, i, silu(held + rising))

    def step(i, carry):
        conv = convolved(parts, HALO + i, start, links, i, padded, patches, matrix, bias)
        out[i] = x[i] + conv.T
        return carry

    lax.fori_loop(0, count, step, 0)


def exchange_kernel(margins, shared, windows, *refs):
    halos = len(margins)
    total = halos + shared + windows
    given = 2 * halos + shared + 3 * windows
    ins, outs = refs[:total], refs[total : total + given]
    send_halo, recv_halo, send_all, recv_all = refs[total + given :]
    group, member, groups, members = place()
    position = group * members + member
    whole = groups * members
    has_left, has_right = position > 0, position < whole - 1
    has_low, has_high = group > 0, group < groups - 1
    left_at = (jnp.maximum(position - 1, 0) // members, (position + members - 1) % members)
    right_at = (jnp.minimum(position + 1, whole - 1) // members, (position + 1) % members)
    low_at = (jnp.maximum(group - 1, 0), members - 1)
    high_at = (jnp.minimum(group + 1, groups - 1), 0)

    barrier = pltpu.get_barrier_semaphore()

    def greet(where):
        pl.semaphore_signal(barrier, inc=1, device_id=where, device_id_type=MESH)

    count = jnp.int32(0)
    if halos:
        pl.when(has_left)(lambda: greet(left_at))
        pl.when(has_right)(lambda: greet(right_at))
        count = count + jnp.where(has_left, 1, 0) + jnp.where(has_right, 1, 0)
    if shared or windows:
        for k in range(1, members):
            greet((group, (member + k) % members))
        for k in range(members):
            pl.when((member == 0) & has_low)(lambda k=k: greet((low_at[0], k)))
            pl.when((member == members - 1) & has_high)(lambda k=k: greet((high_at[0], k)))
        count = count + (members - 1) + jnp.where(has_low, 1, 0) + jnp.where(has_high, 1, 0)
    pl.semaphore_wait(barrier, count)

    def remote(src, dst, send, recv, where):
        return pltpu.make_async_remote_copy(
            src_ref=src, dst_ref=dst, send_sem=send, recv_sem=recv,
            device_id=where, device_id_type=MESH,
        )

    def parts_of(a):
        src = ins[halos + a]
        if a < shared:
            out = outs[2 * halos + a]
            return (
                lambda to: src, src, src,
                lambda by: out.at[members + by],
                lambda by: out.at[by],
                lambda by: out.at[2 * members + by],
            )
        window, low, high = outs[2 * halos + shared + 3 * (a - shared) :][:3]
        span = window.shape[1]
        each = span - 2 * HALO
        bricks = src.shape[0] - 2 * HALO
        return (
            lambda to: src.at[pl.ds(to * each, span)],
            src.at[bricks : bricks + HALO],
            src.at[HALO : 2 * HALO],
            lambda by: window.at[by],
            lambda by: low.at[by],
            lambda by: high.at[by],
        )

    def each(action):
        for a in range(shared + windows):
            own, up, down, here, below, above = parts_of(a)
            sends, recvs = send_all.at[a], recv_all.at[a]
            for k in range(1, members):
                other = (member + k) % members
                by = member if action == "start" else other
                copy = remote(
                    own(other), here(by), sends.at[k], recvs.at[members + by], (group, other)
                )
                copy.start() if action == "start" else copy.wait()
            to_high = remote(up, below(member), sends.at[0], recvs.at[member], high_at)
            to_low = remote(
                down, above(member), sends.at[members], recvs.at[2 * members + member], low_at
            )
            if action == "start":
                pl.when(has_high)(to_high.start)
                pl.when(has_low)(to_low.start)
            else:
                pl.when(has_high)(to_high.wait_send)
                pl.when(has_low)(to_low.wait_send)
                for k in range(members):
                    from_low = remote(up, below(k), sends.at[0], recvs.at[k], low_at)
                    from_high = remote(
                        down, above(k), sends.at[0], recvs.at[2 * members + k], high_at
                    )
                    pl.when((member == 0) & has_low)(from_low.wait_recv)
                    pl.when((member == members - 1) & has_high)(from_high.wait_recv)
        for a, margin in enumerate(margins):
            src, before, after = ins[a], outs[2 * a], outs[2 * a + 1]
            length = src.shape[0]
            to_right = remote(
                src.at[length - margin : length], before, send_halo.at[a, 0],
                recv_halo.at[a, 0], right_at,
            )
            to_left = remote(
                src.at[0:margin], after, send_halo.at[a, 1], recv_halo.at[a, 1], left_at
            )
            if action == "start":
                pl.when(has_right)(to_right.start)
                pl.when(has_left)(to_left.start)
            else:
                pl.when(has_right)(to_right.wait_send)
                pl.when(has_left)(to_left.wait_send)
                pl.when(has_left)(to_right.wait_recv)
                pl.when(has_right)(to_left.wait_recv)

    each("start")
    for a in range(shared):
        outs[2 * halos + a][members + member] = ins[halos + a][...]
    for a in range(shared, shared + windows):
        window, src = outs[2 * halos + shared + 3 * (a - shared)], ins[halos + a]
        span = window.shape[1]
        window[member] = src[pl.ds(member * (span - 2 * HALO), span)]
    each("wait")


def exchange(halos, shared, windows, number):
    members = lax.axis_size("dev")
    shapes = []
    for array, margin in halos:
        shapes += [jax.ShapeDtypeStruct((margin,) + array.shape[1:], array.dtype)] * 2
    for array in shared:
        shapes.append(jax.ShapeDtypeStruct((3 * members,) + array.shape, array.dtype))
    for array in windows:
        span = (array.shape[0] - 2 * HALO) // members + 2 * HALO
        for rows in (span, HALO, HALO):
            shapes.append(
                jax.ShapeDtypeStruct((members, rows) + array.shape[1:], array.dtype)
            )
    total = len(halos) + len(shared) + len(windows)
    vmem = pl.BlockSpec(memory_space=pltpu.VMEM)
    halo_count, share_count = max(len(halos), 1), max(len(shared) + len(windows), 1)
    return pl.pallas_call(
        functools.partial(exchange_kernel, [m for _, m in halos], len(shared), len(windows)),
        out_shape=shapes,
        in_specs=[vmem] * total,
        out_specs=[vmem] * len(shapes),
        scratch_shapes=[
            pltpu.SemaphoreType.DMA((halo_count, 2)),
            pltpu.SemaphoreType.DMA((halo_count, 2)),
            pltpu.SemaphoreType.DMA((share_count, members + 1)),
            pltpu.SemaphoreType.DMA((share_count, 3 * members)),
        ],
        name=f"exchange_{number}",
        compiler_params=pltpu.CompilerParams(
            collective_id=number, has_side_effects=True, vmem_limit_bytes=LIMIT
        ),
    )(*[a for a, _ in halos], *shared, *windows)


def local(kernel, shapes, args, scalars, scratch):
    vmem = pl.BlockSpec(memory_space=pltpu.VMEM)
    smem = pl.BlockSpec(memory_space=pltpu.SMEM)
    return pl.pallas_call(
        kernel,
        out_shape=shapes,
        in_specs=[smem if i in scalars else vmem for i in range(len(args))],
        out_specs=[vmem] * len(shapes),
        scratch_shapes=scratch,
        name=kernel.__name__,
        compiler_params=pltpu.CompilerParams(vmem_limit_bytes=LIMIT),
    )(*args)


def conv_scratch(bricks, channels):
    width = 2 * channels
    return [
        pltpu.VMEM((bricks, SIDE, SIDE, SIDE, width), F32),
        pltpu.VMEM((3, PADDED, PADDED, SIDE, width), F32),
        pltpu.VMEM((VOX, 27 * width), BF16),
        pltpu.VMEM((width, 27 * width), BF16),
    ]


def per_device(
    x, fine_links, parent_codes, coarse_links,
    in_weight, in_bias, down, one_weight, one_bias, two_weight, two_bias, up, out_weight, out_bias,
):
    count, channels = x.shape[0], x.shape[1]
    slots, wide = coarse_links.shape[0], one_bias.shape[0]
    sized = lambda *shape: jax.ShapeDtypeStruct(shape, F32)
    row = lambda bias: bias.reshape(1, -1)
    code_block = jnp.pad(parent_codes.reshape(1, -1), ((0, 7), (0, 128 - count)))
    members = lax.axis_size("dev")
    flat = (FINE_ROWS // 2, 2 * channels)
    (packed,) = local(pack_kernel, [sized(count, *flat)], [x], (), [])
    left, right, codes = exchange([(packed, HALO)], [code_block], [], 1)
    codes = codes.reshape(-1, 128)
    hidden, packed, pooled = local(
        first_kernel,
        [
            sized(count, VOX // 2, 2 * channels),
            sized(count, *flat),
            sized(count, OCT // 2, 2 * channels),
        ],
        [x, left, right, fine_links, in_weight, row(in_bias)],
        (3,),
        conv_scratch(count + 2 * HALO, channels),
    )
    hidden_left, hidden_right, pooled = exchange([(packed, HALO)], [pooled], [], 2)
    first, packed = local(
        second_kernel,
        [sized(slots, VOX, wide), sized(slots, COARSE_ROWS, wide)],
        [pooled, codes, coarse_links, down.T, one_weight, row(one_bias)],
        (1, 2),
        [pltpu.VMEM((3 * slots * 8, OCT, channels), F32)] + conv_scratch(3 * slots, wide),
    )
    first_left, first_right = exchange([(packed, slots)], [], [], 3)
    (wanted,) = local(
        third_kernel,
        [sized(members * count + 2 * HALO, OCT // 2, 2 * channels)],
        [first, first_left, first_right, coarse_links, codes, two_weight, row(two_bias), up],
        (3, 4),
        [pltpu.VMEM((slots * 8, OCT // 2, 2 * channels), F32)] + conv_scratch(3 * slots, wide),
    )
    window, low, high = exchange([], [], [wanted], 4)
    (out,) = local(
        fourth_kernel,
        [sized(count, channels, VOX)],
        [x, hidden, hidden_left, hidden_right, window, low, high, fine_links, out_weight,
         row(out_bias)],
        (7,),
        conv_scratch(count + 2 * HALO, channels),
    )
    return out


def solution(mesh):
    bricks = P(("grp", "dev"), None, None)
    rows = P(("grp", "dev"), None)
    placed = (bricks, rows, P(("grp", "dev")), rows) + (P(),) * 10
    return jax.shard_map(
        per_device, mesh=mesh, in_specs=placed, out_specs=bricks, check_vma=False
    )
```
